128 devices in a mesh: dp: 16 (over y_lo, z, core), tensor: 8 (over x, y_hi).
Axes of the slice: x: 4, y: 4 (y_hi: 2, y_lo: 2; y = y_hi * 2 + y_lo), z: 4, core: 2. Of those that a mesh axis runs over, the one named last changes fastest.
Arguments:
- queries: bfloat16 [16384, 4096], P('dp')
- keys: bfloat16 [16384, 4096], P('dp')
- projection: bfloat16 [4096, 1024], P(None, 'tensor'), may hold values from -0.09375 to 0.09375
- positives: int32 [16, 1024], P('dp'), may hold values from 0 to 1023, each once within a row
Outputs:
- pair_loss: float32 [16384], P(('dp', 'tensor'))
- grad_queries: float32 [16384, 1024], P(('dp', 'tensor'))
- grad_keys: float32 [16384, 1024], P(('dp', 'tensor'))
The draws below stay inside these ranges and needn't reach their ends.
Inputs may be any that keep to these rules, and one draw needn't show every extreme that they name: Each row of positives holds every number of 0 to 1023 once.
All inputs are finite; a program needn't handle non-finite values.
Results may differ from the reference program's by a relative error of at most 0.0069.
Values may be sent and summed in bfloat16 or wider, within the bound.
No kernel may reach another device: no remote copies, remote signals or barrier semaphores. Data moves between devices by JAX's collectives and lax.ppermute only.
A program may use at most 128 MiB of HBM per device.

```python
import jax
import jax.numpy as jnp
from jax import lax

D = 4096
E = 1024
ROWS = 1024
PAIRS = 16384
N_DP = 16


def draw_both(seeded):
    mixed = jax.random.fold_in(seeded, 4093)
    subkeys = jax.random.split(mixed, 2)
    query_draw = jax.random.normal(subkeys[0], (PAIRS, D), jnp.float32)
    key_draw = jax.random.normal(subkeys[1], (PAIRS, D), jnp.float32)
    return (query_draw, key_draw)


def draw_queries(key, part):
    return draw_both(key)[0].astype(jnp.bfloat16)


def draw_keys(key, part):
    return draw_both(key)[1].astype(jnp.bfloat16)


def levels(own_key, dims, shards, smallest, top_value):
    factor_of = 1.0
    for dim, shards_of in shards:
        draws = jax.random.uniform(jax.random.fold_in(jax.random.fold_in(own_key, 6), dim), (shards_of,), jnp.float32, smallest / len(shards), top_value / len(shards))
        factor_of = factor_of * jnp.repeat(jnp.exp(draws), dims[dim] // shards_of).reshape((-1,) + (1,) * (len(dims) - 1 - dim))
    return factor_of


def centred(rng, shape, width, bound, shards=(), kind=jnp.bfloat16):
    factor_of = levels(rng, shape, shards, -0.22, 0.18) if shards else 1.0
    values = jax.random.normal(rng, shape, jnp.float32) * width * factor_of
    return jnp.minimum(jnp.maximum(values, -bound), bound).astype(kind)


def setup_inputs(seed: int = 0) -> dict:
    arg_keys = jax.random.split(jax.random.key(seed), 5)
    return {
        "queries": draw_queries(jax.random.fold_in(arg_keys[4], 71), 0),
        "keys": draw_keys(jax.random.fold_in(arg_keys[4], 71), 0),
        "projection": centred(arg_keys[2], (D, E), D ** -0.5, 0.09375, ((1, 8),)),
        "positives": jax.vmap(lambda own: jax.random.permutation(own, ROWS))(jax.random.split(arg_keys[3], N_DP)).reshape((N_DP, ROWS)).astype(jnp.int32),
    }


SCALE = 100.0
EPSILON = 1e-06

def normalize(embedding):
    entries = embedding.astype(jnp.float32)
    magnitude = jnp.sqrt(lax.optimization_barrier(jnp.sum(entries * entries, axis=1, keepdims=True)) + EPSILON)
    return (entries / magnitude, magnitude)

def unnormalize(grad_unit, unit_rows, magnitude):
    return (grad_unit - unit_rows * lax.optimization_barrier(jnp.sum(unit_rows * grad_unit, axis=1, keepdims=True))) / magnitude

def reference(queries, keys, projection, positives):
    query_proj = jnp.dot(queries, projection, preferred_element_type=jnp.float32).astype(jnp.bfloat16)
    key_proj = jnp.dot(keys, projection, preferred_element_type=jnp.float32).astype(jnp.bfloat16)
    query_unit, query_mag = normalize(query_proj)
    key_unit, key_mag = normalize(key_proj)
    query_hat = query_unit.astype(jnp.bfloat16)
    key_hat = key_unit.astype(jnp.bfloat16)
    offsets = (jnp.arange(N_DP, dtype=jnp.int32) * ROWS)[:, None]
    targets = (positives.astype(jnp.int32) + offsets).reshape(N_DP, ROWS)
    blocks = query_hat.reshape(N_DP, ROWS, E)
    columns = jnp.arange(PAIRS, dtype=jnp.int32)[None, :]

    def one_block(grad_key_hat, inputs):
        query_block, target = inputs
        scores = SCALE * lax.dot_general(query_block, key_hat, (((1,), (1,)), ((), ())), preferred_element_type=jnp.float32)
        row_max = lax.optimization_barrier(jnp.max(scores, axis=1))
        log_total = row_max + jnp.log(lax.optimization_barrier(jnp.sum(jnp.exp(scores - row_max[:, None]), axis=1)))
        positive_mask = (columns == target[:, None]).astype(jnp.float32)
        matched = lax.optimization_barrier(jnp.sum(scores * positive_mask, axis=1))
        weights = (jnp.exp(scores - log_total[:, None]) - positive_mask).astype(jnp.bfloat16)
        grad_q = SCALE * jnp.dot(weights, key_hat, preferred_element_type=jnp.float32)
        grad_key_hat = grad_key_hat + SCALE * lax.dot_general(weights, query_block, (((0,), (0,)), ((), ())), preferred_element_type=jnp.float32)
        return (grad_key_hat, (log_total - matched, grad_q))
    grad_key_hat, (losses, grad_query_hat) = lax.scan(one_block, jnp.zeros((PAIRS, E), jnp.float32), (blocks, targets))
    pair_loss = losses.reshape(PAIRS)
    grad_queries = unnormalize(grad_query_hat.reshape(PAIRS, E), query_unit, query_mag)
    grad_keys = unnormalize(grad_key_hat, key_unit, key_mag)
    return (pair_loss, grad_queries, grad_keys)
```

```python
import jax
import jax.numpy as jnp
from jax import lax
from jax.sharding import PartitionSpec as P

SCALE = 100.0
EPSILON = 1e-06


def normalize(embedding):
    entries = embedding.astype(jnp.float32)
    magnitude = jnp.sqrt(jnp.sum(entries * entries, axis=1, keepdims=True) + EPSILON)
    return (entries / magnitude, magnitude)


def unnormalize(grad_unit, unit_rows, magnitude):
    return (
        grad_unit - unit_rows * jnp.sum(unit_rows * grad_unit, axis=1, keepdims=True)
    ) / magnitude


def body(queries, keys, projection, positives):
    rows = queries.shape[0]
    group_count = lax.axis_size("tensor")
    group_index = lax.axis_index("tensor")
    block_index = lax.axis_index("dp")
    slice_rows = rows // group_count
    row_start = group_index * slice_rows

    query_part = jnp.dot(queries, projection, preferred_element_type=jnp.float32).astype(jnp.bfloat16)
    key_part = jnp.dot(keys, projection, preferred_element_type=jnp.float32).astype(jnp.bfloat16)
    query_full = lax.all_gather(query_part, "tensor", axis=1, tiled=True)
    key_rows = lax.all_to_all(key_part, "tensor", 0, 1, tiled=True)

    query_unit, query_mag = normalize(query_full)
    queries_hat = query_unit.astype(jnp.bfloat16)
    key_unit, key_mag = normalize(key_rows)
    key_hat = key_unit.astype(jnp.bfloat16)
    keys_all = lax.all_gather(key_hat, "dp", axis=0, tiled=True)

    scores = SCALE * lax.dot_general(
        queries_hat, keys_all, (((1,), (1,)), ((), ())), preferred_element_type=jnp.float32
    )
    local_pos = positives[0] - row_start
    column = block_index * slice_rows + local_pos
    valid = (local_pos >= 0) & (local_pos < slice_rows)
    column = jnp.where(valid, column, -1)
    positive_mask = (
        lax.broadcasted_iota(jnp.int32, scores.shape, 1) == column[:, None]
    ).astype(jnp.float32)
    row_max = jnp.max(scores, axis=1)
    row_sum = jnp.sum(jnp.exp(scores - row_max[:, None]), axis=1)
    matched = jnp.sum(scores * positive_mask, axis=1)

    stats = lax.all_gather(jnp.stack([row_max, row_sum, matched]), "tensor", axis=0)
    all_max = jnp.max(stats[:, 0], axis=0)
    total = jnp.sum(stats[:, 1] * jnp.exp(stats[:, 0] - all_max[None, :]), axis=0)
    matched = jnp.sum(stats[:, 2], axis=0)
    log_total = all_max + jnp.log(total)
    pair_loss = lax.dynamic_slice_in_dim(log_total - matched, row_start, slice_rows, 0)

    weights = (jnp.exp(scores - log_total[:, None]) - positive_mask).astype(jnp.bfloat16)
    grad_k = SCALE * lax.dot_general(
        weights, queries_hat, (((0,), (0,)), ((), ())), preferred_element_type=jnp.float32
    )
    grad_key_hat = lax.psum_scatter(grad_k, "dp", scatter_dimension=0, tiled=True)
    grad_q = SCALE * jnp.dot(weights, keys_all, preferred_element_type=jnp.float32)
    grad_rows = lax.psum_scatter(grad_q, "tensor", scatter_dimension=0, tiled=True)

    unit_rows = lax.dynamic_slice_in_dim(query_unit, row_start, slice_rows, 0)
    magnitude_rows = lax.dynamic_slice_in_dim(query_mag, row_start, slice_rows, 0)
    grad_queries = unnormalize(grad_rows, unit_rows, magnitude_rows)
    grad_keys = unnormalize(grad_key_hat, key_unit, key_mag)
    return (pair_loss, grad_queries, grad_keys)


def solution(mesh):
    in_specs = (P("dp", None), P("dp", None), P(None, "tensor"), P("dp", None))
    out_specs = (P(("dp", "tensor")), P(("dp", "tensor"), None), P(("dp", "tensor"), None))
    return jax.shard_map(body, mesh=mesh, in_specs=in_specs, out_specs=out_specs, check_vma=False)
```

```python
import jax
import jax.numpy as jnp
from jax import lax
from jax.sharding import PartitionSpec as P

SCALE = 100.0
EPSILON = 1e-06


def normalize(embedding):
    entries = embedding.astype(jnp.float32)
    magnitude = jnp.sqrt(jnp.sum(entries * entries, axis=1, keepdims=True) + EPSILON)
    return (entries / magnitude, magnitude)


def unnormalize(grad_unit, unit_rows, magnitude):
    return (
        grad_unit - unit_rows * jnp.sum(unit_rows * grad_unit, axis=1, keepdims=True)
    ) / magnitude


def from_peers(value, axis, count):
    return [value] + [
        lax.ppermute(value, axis, [(source, (source - step) % count) for source in range(count)])
        for step in range(1, count)
    ]


def gather_columns(value, axis, count):
    received = from_peers(value, axis, count)
    joined = jnp.concatenate(received, axis=1)
    return jnp.roll(joined, lax.axis_index(axis) * value.shape[1], axis=1)


def exchange_rows(value, axis, count):
    index = lax.axis_index(axis)
    size = value.shape[0] // count
    received = [lax.dynamic_slice_in_dim(value, index * size, size, 0)]
    for step in range(1, count):
        chunk = lax.dynamic_slice_in_dim(value, ((index - step) % count) * size, size, 0)
        received.append(lax.ppermute(chunk, axis, [(source, (source - step) % count) for source in range(count)]))
    joined = jnp.concatenate(received, axis=1)
    return jnp.roll(joined, index * value.shape[1], axis=1)


def scatter_sum(value, axis, count):
    index = lax.axis_index(axis)
    size = value.shape[0] // count
    total = lax.dynamic_slice_in_dim(value, index * size, size, 0)
    for step in range(1, count):
        chunk = lax.dynamic_slice_in_dim(value, ((index + step) % count) * size, size, 0)
        total = total + lax.ppermute(chunk, axis, [(source, (source + step) % count) for source in range(count)])
    return total


def body(queries, keys, projection, positives):
    rows = queries.shape[0]
    group_count = lax.axis_size("tensor")
    group_index = lax.axis_index("tensor")
    block_index = lax.axis_index("dp")
    slice_rows = rows // group_count
    row_start = group_index * slice_rows

    key_part = jnp.dot(keys, projection, preferred_element_type=jnp.float32).astype(jnp.bfloat16)
    key_rows = exchange_rows(key_part, "tensor", group_count)
    query_part = jnp.dot(queries, projection, preferred_element_type=jnp.float32).astype(jnp.bfloat16)
    query_full = gather_columns(query_part, "tensor", group_count)

    query_unit, query_mag = normalize(query_full)
    queries_hat = query_unit.astype(jnp.bfloat16)
    key_unit, key_mag = normalize(key_rows)
    key_hat = key_unit.astype(jnp.bfloat16)
    keys_all = lax.all_gather(key_hat, "dp", axis=0, tiled=True)

    scores = SCALE * lax.dot_general(
        queries_hat, keys_all, (((1,), (1,)), ((), ())), preferred_element_type=jnp.float32
    )
    local_pos = positives[0] - row_start
    column = block_index * slice_rows + local_pos
    valid = (local_pos >= 0) & (local_pos < slice_rows)
    column = jnp.where(valid, column, -1)
    positive_mask = (
        lax.broadcasted_iota(jnp.int32, scores.shape, 1) == column[:, None]
    ).astype(jnp.float32)
    row_max = jnp.max(scores, axis=1)
    row_sum = jnp.sum(jnp.exp(scores - row_max[:, None]), axis=1)
    matched = jnp.sum(scores * positive_mask, axis=1)

    stats = jnp.stack(from_peers(jnp.stack([row_max, row_sum, matched]), "tensor", group_count))
    all_max = jnp.max(stats[:, 0], axis=0)
    total = jnp.sum(stats[:, 1] * jnp.exp(stats[:, 0] - all_max[None, :]), axis=0)
    matched = jnp.sum(stats[:, 2], axis=0)
    log_total = all_max + jnp.log(total)
    pair_loss = lax.dynamic_slice_in_dim(log_total - matched, row_start, slice_rows, 0)

    weights = (jnp.exp(scores - log_total[:, None]) - positive_mask).astype(jnp.bfloat16)
    grad_k = SCALE * lax.dot_general(
        weights, queries_hat, (((0,), (0,)), ((), ())), preferred_element_type=jnp.float32
    )
    grad_key_hat = lax.psum_scatter(grad_k, "dp", scatter_dimension=0, tiled=True)
    grad_q = SCALE * jnp.dot(weights, keys_all, preferred_element_type=jnp.float32)
    grad_rows = scatter_sum(grad_q, "tensor", group_count)

    unit_rows = lax.dynamic_slice_in_dim(query_unit, row_start, slice_rows, 0)
    magnitude_rows = lax.dynamic_slice_in_dim(query_mag, row_start, slice_rows, 0)
    grad_queries = unnormalize(grad_rows, unit_rows, magnitude_rows)
    grad_keys = unnormalize(grad_key_hat, key_unit, key_mag)
    return (pair_loss, grad_queries, grad_keys)


def solution(mesh):
    in_specs = (P("dp", None), P("dp", None), P(None, "tensor"), P("dp", None))
    out_specs = (P(("dp", "tensor")), P(("dp", "tensor"), None), P(("dp", "tensor"), None))
    return jax.shard_map(body, mesh=mesh, in_specs=in_specs, out_specs=out_specs, check_vma=False)
```

```python
import jax
import jax.numpy as jnp
from jax import lax
from jax.sharding import PartitionSpec as P

SCALE = 100.0
EPSILON = 1e-06


def normalize(embedding):
    entries = embedding.astype(jnp.float32)
    magnitude = jnp.sqrt(jnp.sum(entries * entries, axis=1, keepdims=True) + EPSILON)
    return (entries / magnitude, magnitude)


def unnormalize(grad_unit, unit_rows, magnitude):
    return (
        grad_unit - unit_rows * jnp.sum(unit_rows * grad_unit, axis=1, keepdims=True)
    ) / magnitude


def unrotate(pieces, index, width):
    count = len(pieces)
    joined = jnp.concatenate(pieces + pieces, axis=1)
    return lax.dynamic_slice_in_dim(joined, (count - index) * width, count * width, 1)


def exchange_projections(query_part, key_part, axis, count):
    index = lax.axis_index(axis)
    rows, width = query_part.shape
    size = rows // count
    received = [jnp.concatenate([query_part, lax.dynamic_slice_in_dim(key_part, index * size, size, 0)])]
    for step in range(1, count):
        chunk = lax.dynamic_slice_in_dim(key_part, ((index - step) % count) * size, size, 0)
        outgoing = jnp.concatenate([query_part, chunk])
        received.append(lax.ppermute(outgoing, axis, [(source, (source - step) % count) for source in range(count)]))
    query_full = unrotate([piece[:rows] for piece in received], index, width)
    key_rows = unrotate([piece[rows:] for piece in received], index, width)
    return query_full, key_rows


def combine_stats(earlier, latter):
    new_max = jnp.maximum(earlier[0], latter[0])
    total = earlier[1] * jnp.exp(earlier[0] - new_max) + latter[1] * jnp.exp(latter[0] - new_max)
    return jnp.stack([new_max, total, earlier[2] + latter[2]])


def all_stats(stats, axis, count):
    step = 1
    while step < count:
        partner = lax.ppermute(stats, axis, [(source, source ^ step) for source in range(count)])
        stats = combine_stats(stats, partner)
        step *= 2
    return stats


def scatter_sum(value, axis, count):
    index = lax.axis_index(axis)
    size = value.shape[0] // count
    total = lax.dynamic_slice_in_dim(value, index * size, size, 0)
    for step in range(1, count):
        chunk = lax.dynamic_slice_in_dim(value, ((index + step) % count) * size, size, 0)
        total = total + lax.ppermute(chunk, axis, [(source, (source + step) % count) for source in range(count)])
    return total


def body(queries, keys, projection, positives):
    rows = queries.shape[0]
    group_count = lax.axis_size("tensor")
    group_index = lax.axis_index("tensor")
    block_index = lax.axis_index("dp")
    slice_rows = rows // group_count
    row_start = group_index * slice_rows

    key_part = jnp.dot(keys, projection, preferred_element_type=jnp.float32).astype(jnp.bfloat16)
    query_part = jnp.dot(queries, projection, preferred_element_type=jnp.float32).astype(jnp.bfloat16)
    query_full, key_rows = exchange_projections(query_part, key_part, "tensor", group_count)

    query_unit, query_mag = normalize(query_full)
    queries_hat = query_unit.astype(jnp.bfloat16)
    key_unit, key_mag = normalize(key_rows)
    key_hat = key_unit.astype(jnp.bfloat16)
    keys_all = lax.all_gather(key_hat, "dp", axis=0, tiled=True)

    scores = SCALE * lax.dot_general(
        queries_hat, keys_all, (((1,), (1,)), ((), ())), preferred_element_type=jnp.float32
    )
    local_pos = positives[0] - row_start
    column = block_index * slice_rows + local_pos
    valid = (local_pos >= 0) & (local_pos < slice_rows)
    column = jnp.where(valid, column, -1)
    positive_mask = (
        lax.broadcasted_iota(jnp.int32, scores.shape, 1) == column[:, None]
    ).astype(jnp.float32)
    row_max = jnp.max(scores, axis=1)
    row_sum = jnp.sum(jnp.exp(scores - row_max[:, None]), axis=1)
    matched = jnp.sum(scores * positive_mask, axis=1)

    stats = all_stats(jnp.stack([row_max, row_sum, matched]), "tensor", group_count)
    matched = stats[2]
    log_total = stats[0] + jnp.log(stats[1])
    pair_loss = lax.dynamic_slice_in_dim(log_total - matched, row_start, slice_rows, 0)

    weights = (jnp.exp(scores - log_total[:, None]) - positive_mask).astype(jnp.bfloat16)
    grad_k = SCALE * lax.dot_general(
        weights, queries_hat, (((0,), (0,)), ((), ())), preferred_element_type=jnp.float32
    )
    grad_key_hat = lax.psum_scatter(grad_k, "dp", scatter_dimension=0, tiled=True)
    grad_q = SCALE * jnp.dot(weights, keys_all, preferred_element_type=jnp.float32)
    grad_rows = scatter_sum(grad_q, "tensor", group_count)

    unit_rows = lax.dynamic_slice_in_dim(query_unit, row_start, slice_rows, 0)
    magnitude_rows = lax.dynamic_slice_in_dim(query_mag, row_start, slice_rows, 0)
    grad_queries = unnormalize(grad_rows, unit_rows, magnitude_rows)
    grad_keys = unnormalize(grad_key_hat, key_unit, key_mag)
    return (pair_loss, grad_queries, grad_keys)


def solution(mesh):
    in_specs = (P("dp", None), P("dp", None), P(None, "tensor"), P("dp", None))
    out_specs = (P(("dp", "tensor")), P(("dp", "tensor"), None), P(("dp", "tensor"), None))
    return jax.shard_map(body, mesh=mesh, in_specs=in_specs, out_specs=out_specs, check_vma=False)
```

```python
import jax
import jax.numpy as jnp
from jax import lax
from jax.sharding import PartitionSpec as P

SCALE = 100.0
EPSILON = 1e-06


def normalize(embedding):
    entries = embedding.astype(jnp.float32)
    magnitude = jnp.sqrt(jnp.sum(entries * entries, axis=1, keepdims=True) + EPSILON)
    return (entries / magnitude, magnitude)


def unnormalize(grad_unit, unit_rows, magnitude):
    return (
        grad_unit - unit_rows * jnp.sum(unit_rows * grad_unit, axis=1, keepdims=True)
    ) / magnitude


def unrotate(pieces, index, width):
    count = len(pieces)
    joined = jnp.concatenate(pieces + pieces, axis=1)
    return lax.dynamic_slice_in_dim(joined, (count - index) * width, count * width, 1)


def exchange_projections(query_part, key_part, axis, count):
    index = lax.axis_index(axis)
    rows, width = query_part.shape
    size = rows // count
    received = [jnp.concatenate([query_part, lax.dynamic_slice_in_dim(key_part, index * size, size, 0)])]
    for step in range(1, count):
        chunk = lax.dynamic_slice_in_dim(key_part, ((index - step) % count) * size, size, 0)
        outgoing = jnp.concatenate([query_part, chunk])
        received.append(lax.ppermute(outgoing, axis, [(source, (source - step) % count) for source in range(count)]))
    query_full = unrotate([piece[:rows] for piece in received], index, width)
    key_rows = unrotate([piece[rows:] for piece in received], index, width)
    return query_full, key_rows


def combine_stats(earlier, latter):
    new_max = jnp.maximum(earlier[0], latter[0])
    total = earlier[1] * jnp.exp(earlier[0] - new_max) + latter[1] * jnp.exp(latter[0] - new_max)
    return jnp.stack([new_max, total, earlier[2] + latter[2]])


def all_stats(stats, axis, count):
    step = 1
    while step < count:
        partner = lax.ppermute(stats, axis, [(source, source ^ step) for source in range(count)])
        stats = combine_stats(stats, partner)
        step *= 2
    return stats


def scatter_sum(value, axis, count):
    index = lax.axis_index(axis)
    size = value.shape[0] // count
    lanes = 2
    rings = count // lanes
    ring_index = index // lanes
    lane = index % lanes
    part = lax.dynamic_slice_in_dim(value, ring_index * lanes * size, lanes * size, 0)
    for step in range(1, rings):
        chunk = lax.dynamic_slice_in_dim(value, ((ring_index + step) % rings) * lanes * size, lanes * size, 0)
        pairs = [(source, ((source // lanes + step) % rings) * lanes + source % lanes) for source in range(count)]
        part = part + lax.ppermute(chunk, axis, pairs)
    other = lax.dynamic_slice_in_dim(part, (1 - lane) * size, size, 0)
    own = lax.dynamic_slice_in_dim(part, lane * size, size, 0)
    return own + lax.ppermute(other, axis, [(source, source ^ 1) for source in range(count)])


def body(queries, keys, projection, positives):
    rows = queries.shape[0]
    group_count = lax.axis_size("tensor")
    group_index = lax.axis_index("tensor")
    block_index = lax.axis_index("dp")
    slice_rows = rows // group_count
    row_start = group_index * slice_rows

    key_part = jnp.dot(keys, projection, preferred_element_type=jnp.float32).astype(jnp.bfloat16)
    query_part = jnp.dot(queries, projection, preferred_element_type=jnp.float32).astype(jnp.bfloat16)
    query_full, key_rows = exchange_projections(query_part, key_part, "tensor", group_count)

    query_unit, query_mag = normalize(query_full)
    queries_hat = query_unit.astype(jnp.bfloat16)
    key_unit, key_mag = normalize(key_rows)
    key_hat = key_unit.astype(jnp.bfloat16)
    keys_all = lax.all_gather(key_hat, "dp", axis=0, tiled=True)

    scores = SCALE * lax.dot_general(
        queries_hat, keys_all, (((1,), (1,)), ((), ())), preferred_element_type=jnp.float32
    )
    local_pos = positives[0] - row_start
    column = block_index * slice_rows + local_pos
    valid = (local_pos >= 0) & (local_pos < slice_rows)
    column = jnp.where(valid, column, -1)
    positive_mask = (
        lax.broadcasted_iota(jnp.int32, scores.shape, 1) == column[:, None]
    ).astype(jnp.float32)
    row_max = jnp.max(scores, axis=1)
    row_sum = jnp.sum(jnp.exp(scores - row_max[:, None]), axis=1)
    matched = jnp.sum(scores * positive_mask, axis=1)

    stats = all_stats(jnp.stack([row_max, row_sum, matched]), "tensor", group_count)
    matched = stats[2]
    log_total = stats[0] + jnp.log(stats[1])
    pair_loss = lax.dynamic_slice_in_dim(log_total - matched, row_start, slice_rows, 0)

    weights = (jnp.exp(scores - log_total[:, None]) - positive_mask).astype(jnp.bfloat16)
    grad_k = SCALE * lax.dot_general(
        weights, queries_hat, (((0,), (0,)), ((), ())), preferred_element_type=jnp.float32
    )
    grad_key_hat = lax.psum_scatter(grad_k, "dp", scatter_dimension=0, tiled=True)
    grad_q = SCALE * jnp.dot(weights, keys_all, preferred_element_type=jnp.float32)
    grad_rows = scatter_sum(grad_q, "tensor", group_count)

    unit_rows = lax.dynamic_slice_in_dim(query_unit, row_start, slice_rows, 0)
    magnitude_rows = lax.dynamic_slice_in_dim(query_mag, row_start, slice_rows, 0)
    grad_queries = unnormalize(grad_rows, unit_rows, magnitude_rows)
    grad_keys = unnormalize(grad_key_hat, key_unit, key_mag)
    return (pair_loss, grad_queries, grad_keys)


def solution(mesh):
    in_specs = (P("dp", None), P("dp", None), P(None, "tensor"), P("dp", None))
    out_specs = (P(("dp", "tensor")), P(("dp", "tensor"), None), P(("dp", "tensor"), None))
    return jax.shard_map(body, mesh=mesh, in_specs=in_specs, out_specs=out_specs, check_vma=False)
```

```python
import jax
import jax.numpy as jnp
from jax import lax
from jax.sharding import PartitionSpec as P

SCALE = 100.0
EPSILON = 1e-06


def normalize(embedding):
    entries = embedding.astype(jnp.float32)
    magnitude = jnp.sqrt(jnp.sum(entries * entries, axis=1, keepdims=True) + EPSILON)
    return (entries / magnitude, magnitude)


def unnormalize(grad_unit, unit_rows, magnitude):
    return (
        grad_unit - unit_rows * jnp.sum(unit_rows * grad_unit, axis=1, keepdims=True)
    ) / magnitude


def unrotate(pieces, index, width):
    count = len(pieces)
    joined = jnp.concatenate(pieces + pieces, axis=1)
    return lax.dynamic_slice_in_dim(joined, (count - index) * width, count * width, 1)


def exchange_rows(value, axis, count):
    index = lax.axis_index(axis)
    size = value.shape[0] // count
    received = [lax.dynamic_slice_in_dim(value, index * size, size, 0)]
    for step in range(1, count):
        chunk = lax.dynamic_slice_in_dim(value, ((index - step) % count) * size, size, 0)
        received.append(lax.ppermute(chunk, axis, [(source, (source - step) % count) for source in range(count)]))
    return unrotate(received, index, value.shape[1])


def gather_columns(value, axis, count):
    index = lax.axis_index(axis)
    width = value.shape[1]
    lanes = 2
    rings = count // lanes
    ring_index = index // lanes
    lane = index % lanes
    own = [value]
    for step in range(1, rings):
        pairs = [(source, ((source // lanes - step) % rings) * lanes + source % lanes) for source in range(count)]
        own.append(lax.ppermute(value, axis, pairs))
    own = jnp.concatenate(own, axis=1)
    partner = lax.ppermute(own, axis, [(source, source ^ 1) for source in range(count)])
    first = jnp.where(lane == 0, own, partner)
    second = jnp.where(lane == 0, partner, own)
    pieces = []
    for step in range(rings):
        pieces.append(first[:, step * width:(step + 1) * width])
        pieces.append(second[:, step * width:(step + 1) * width])
    return unrotate(pieces, ring_index * lanes, width)


def combine_stats(earlier, latter):
    new_max = jnp.maximum(earlier[0], latter[0])
    total = earlier[1] * jnp.exp(earlier[0] - new_max) + latter[1] * jnp.exp(latter[0] - new_max)
    return jnp.stack([new_max, total, earlier[2] + latter[2]])


def all_stats(stats, axis, count):
    step = 1
    while step < count:
        partner = lax.ppermute(stats, axis, [(source, source ^ step) for source in range(count)])
        stats = combine_stats(stats, partner)
        step *= 2
    return stats


def scatter_sum(value, axis, count):
    index = lax.axis_index(axis)
    size = value.shape[0] // count
    lanes = 2
    rings = count // lanes
    ring_index = index // lanes
    lane = index % lanes
    part = lax.dynamic_slice_in_dim(value, ring_index * lanes * size, lanes * size, 0)
    for step in range(1, rings):
        chunk = lax.dynamic_slice_in_dim(value, ((ring_index + step) % rings) * lanes * size, lanes * size, 0)
        pairs = [(source, ((source // lanes + step) % rings) * lanes + source % lanes) for source in range(count)]
        part = part + lax.ppermute(chunk, axis, pairs)
    other = lax.dynamic_slice_in_dim(part, (1 - lane) * size, size, 0)
    own = lax.dynamic_slice_in_dim(part, lane * size, size, 0)
    return own + lax.ppermute(other, axis, [(source, source ^ 1) for source in range(count)])


def body(queries, keys, projection, positives):
    rows = queries.shape[0]
    group_count = lax.axis_size("tensor")
    group_index = lax.axis_index("tensor")
    block_index = lax.axis_index("dp")
    slice_rows = rows // group_count
    row_start = group_index * slice_rows

    key_part = jnp.dot(keys, projection, preferred_element_type=jnp.float32).astype(jnp.bfloat16)
    query_part = jnp.dot(queries, projection, preferred_element_type=jnp.float32).astype(jnp.bfloat16)
    key_rows = exchange_rows(key_part, "tensor", group_count)
    query_full = gather_columns(query_part, "tensor", group_count)

    query_unit, query_mag = normalize(query_full)
    queries_hat = query_unit.astype(jnp.bfloat16)
    key_unit, key_mag = normalize(key_rows)
    key_hat = key_unit.astype(jnp.bfloat16)
    keys_all = lax.all_gather(key_hat, "dp", axis=0, tiled=True)

    scores = SCALE * lax.dot_general(
        queries_hat, keys_all, (((1,), (1,)), ((), ())), preferred_element_type=jnp.float32
    )
    local_pos = positives[0] - row_start
    column = block_index * slice_rows + local_pos
    valid = (local_pos >= 0) & (local_pos < slice_rows)
    column = jnp.where(valid, column, -1)
    positive_mask = (
        lax.broadcasted_iota(jnp.int32, scores.shape, 1) == column[:, None]
    ).astype(jnp.float32)
    row_max = jnp.max(scores, axis=1)
    row_sum = jnp.sum(jnp.exp(scores - row_max[:, None]), axis=1)
    matched = jnp.sum(scores * positive_mask, axis=1)

    stats = all_stats(jnp.stack([row_max, row_sum, matched]), "tensor", group_count)
    matched = stats[2]
    log_total = stats[0] + jnp.log(stats[1])
    pair_loss = lax.dynamic_slice_in_dim(log_total - matched, row_start, slice_rows, 0)

    weights = (jnp.exp(scores - log_total[:, None]) - positive_mask).astype(jnp.bfloat16)
    grad_k = SCALE * lax.dot_general(
        weights, queries_hat, (((0,), (0,)), ((), ())), preferred_element_type=jnp.float32
    )
    grad_key_hat = lax.psum_scatter(grad_k, "dp", scatter_dimension=0, tiled=True)
    grad_q = SCALE * jnp.dot(weights, keys_all, preferred_element_type=jnp.float32)
    grad_rows = scatter_sum(grad_q, "tensor", group_count)

    unit_rows = lax.dynamic_slice_in_dim(query_unit, row_start, slice_rows, 0)
    magnitude_rows = lax.dynamic_slice_in_dim(query_mag, row_start, slice_rows, 0)
    grad_queries = unnormalize(grad_rows, unit_rows, magnitude_rows)
    grad_keys = unnormalize(grad_key_hat, key_unit, key_mag)
    return (pair_loss, grad_queries, grad_keys)


def solution(mesh):
    in_specs = (P("dp", None), P("dp", None), P(None, "tensor"), P("dp", None))
    out_specs = (P(("dp", "tensor")), P(("dp", "tensor"), None), P(("dp", "tensor"), None))
    return jax.shard_map(body, mesh=mesh, in_specs=in_specs, out_specs=out_specs, check_vma=False)
```

```python
import jax
import jax.numpy as jnp
from jax import lax
from jax.sharding import PartitionSpec as P

SCALE = 100.0
EPSILON = 1e-06


def normalize(embedding):
    entries = embedding.astype(jnp.float32)
    magnitude = jnp.sqrt(jnp.sum(entries * entries, axis=1, keepdims=True) + EPSILON)
    return (entries / magnitude, magnitude)


def unnormalize(grad_unit, unit_rows, magnitude):
    return (
        grad_unit - unit_rows * jnp.sum(unit_rows * grad_unit, axis=1, keepdims=True)
    ) / magnitude


def unrotate(pieces, index, width):
    count = len(pieces)
    joined = jnp.concatenate(pieces + pieces, axis=1)
    return lax.dynamic_slice_in_dim(joined, (count - index) * width, count * width, 1)


def ring_pairs(count, lanes, step):
    rings = count // lanes
    return [(source, ((source // lanes - step) % rings) * lanes + source % lanes) for source in range(count)]


def exchange_rows(value, axis, count, lanes):
    index = lax.axis_index(axis)
    rings = count // lanes
    ring_index = index // lanes
    lane = index % lanes
    size = value.shape[0] // count
    received = [lax.dynamic_slice_in_dim(value, index * size, size, 0)]
    for step in range(1, rings):
        target = ((ring_index - step) % rings) * lanes + lane
        chunk = lax.dynamic_slice_in_dim(value, target * size, size, 0)
        received.append(lax.ppermute(chunk, axis, ring_pairs(count, lanes, step)))
    return unrotate(received, ring_index, value.shape[1])


def gather_columns(value, axis, count, lanes):
    ring_index = lax.axis_index(axis) // lanes
    received = [value] + [
        lax.ppermute(value, axis, ring_pairs(count, lanes, step)) for step in range(1, count // lanes)
    ]
    return unrotate(received, ring_index, value.shape[1])


def combine_stats(earlier, latter):
    new_max = jnp.maximum(earlier[0], latter[0])
    total = earlier[1] * jnp.exp(earlier[0] - new_max) + latter[1] * jnp.exp(latter[0] - new_max)
    return jnp.stack([new_max, total, earlier[2] + latter[2]])


def all_stats(stats, axis, count):
    step = 1
    while step < count:
        partner = lax.ppermute(stats, axis, [(source, source ^ step) for source in range(count)])
        stats = combine_stats(stats, partner)
        step *= 2
    return stats


def scatter_sum(value, axis, count):
    index = lax.axis_index(axis)
    size = value.shape[0] // count
    lanes = 2
    rings = count // lanes
    ring_index = index // lanes
    lane = index % lanes
    part = lax.dynamic_slice_in_dim(value, ring_index * lanes * size, lanes * size, 0)
    for step in range(1, rings):
        chunk = lax.dynamic_slice_in_dim(value, ((ring_index + step) % rings) * lanes * size, lanes * size, 0)
        pairs = [(source, ((source // lanes + step) % rings) * lanes + source % lanes) for source in range(count)]
        part = part + lax.ppermute(chunk, axis, pairs)
    other = lax.dynamic_slice_in_dim(part, (1 - lane) * size, size, 0)
    own = lax.dynamic_slice_in_dim(part, lane * size, size, 0)
    return own + lax.ppermute(other, axis, [(source, source ^ 1) for source in range(count)])


def body(queries, keys, projection, positives):
    rows = queries.shape[0]
    group_count = lax.axis_size("tensor")
    group_index = lax.axis_index("tensor")
    block_index = lax.axis_index("dp")
    slice_rows = rows // group_count
    row_start = group_index * slice_rows

    lanes = 2
    lane = group_index % lanes
    partner_projection = lax.ppermute(projection, "tensor", [(source, source ^ 1) for source in range(group_count)])
    pair_projection = jnp.concatenate(
        [jnp.where(lane == 0, projection, partner_projection), jnp.where(lane == 0, partner_projection, projection)],
        axis=1,
    )
    key_part = jnp.dot(keys, pair_projection, preferred_element_type=jnp.float32).astype(jnp.bfloat16)
    query_part = jnp.dot(queries, pair_projection, preferred_element_type=jnp.float32).astype(jnp.bfloat16)
    key_rows = exchange_rows(key_part, "tensor", group_count, lanes)
    query_full = gather_columns(query_part, "tensor", group_count, lanes)

    query_unit, query_mag = normalize(query_full)
    queries_hat = query_unit.astype(jnp.bfloat16)
    key_unit, key_mag = normalize(key_rows)
    key_hat = key_unit.astype(jnp.bfloat16)
    keys_all = lax.all_gather(key_hat, "dp", axis=0, tiled=True)

    scores = SCALE * lax.dot_general(
        queries_hat, keys_all, (((1,), (1,)), ((), ())), preferred_element_type=jnp.float32
    )
    local_pos = positives[0] - row_start
    column = block_index * slice_rows + local_pos
    valid = (local_pos >= 0) & (local_pos < slice_rows)
    column = jnp.where(valid, column, -1)
    positive_mask = (
        lax.broadcasted_iota(jnp.int32, scores.shape, 1) == column[:, None]
    ).astype(jnp.float32)
    row_max = jnp.max(scores, axis=1)
    row_sum = jnp.sum(jnp.exp(scores - row_max[:, None]), axis=1)
    matched = jnp.sum(scores * positive_mask, axis=1)

    stats = all_stats(jnp.stack([row_max, row_sum, matched]), "tensor", group_count)
    matched = stats[2]
    log_total = stats[0] + jnp.log(stats[1])
    pair_loss = lax.dynamic_slice_in_dim(log_total - matched, row_start, slice_rows, 0)

    weights = (jnp.exp(scores - log_total[:, None]) - positive_mask).astype(jnp.bfloat16)
    grad_k = SCALE * lax.dot_general(
        weights, queries_hat, (((0,), (0,)), ((), ())), preferred_element_type=jnp.float32
    )
    grad_key_hat = lax.psum_scatter(grad_k, "dp", scatter_dimension=0, tiled=True)
    grad_q = SCALE * jnp.dot(weights, keys_all, preferred_element_type=jnp.float32)
    grad_rows = scatter_sum(grad_q, "tensor", group_count)

    unit_rows = lax.dynamic_slice_in_dim(query_unit, row_start, slice_rows, 0)
    magnitude_rows = lax.dynamic_slice_in_dim(query_mag, row_start, slice_rows, 0)
    grad_queries = unnormalize(grad_rows, unit_rows, magnitude_rows)
    grad_keys = unnormalize(grad_key_hat, key_unit, key_mag)
    return (pair_loss, grad_queries, grad_keys)


def solution(mesh):
    in_specs = (P("dp", None), P("dp", None), P(None, "tensor"), P("dp", None))
    out_specs = (P(("dp", "tensor")), P(("dp", "tensor"), None), P(("dp", "tensor"), None))
    return jax.shard_map(body, mesh=mesh, in_specs=in_specs, out_specs=out_specs, check_vma=False)
```

```python
import jax
import jax.numpy as jnp
from jax import lax
from jax.sharding import PartitionSpec as P

SCALE = 100.0
EPSILON = 1e-06


def normalize(embedding):
    entries = embedding.astype(jnp.float32)
    magnitude = jnp.sqrt(jnp.sum(entries * entries, axis=1, keepdims=True) + EPSILON)
    return (entries / magnitude, magnitude)


def unnormalize(grad_unit, unit_rows, magnitude):
    return (
        grad_unit - unit_rows * jnp.sum(unit_rows * grad_unit, axis=1, keepdims=True)
    ) / magnitude


def unrotate(pieces, index, width):
    count = len(pieces)
    return jnp.concatenate([lax.select_n((peer - index) % count, *pieces) for peer in range(count)], axis=1)


def ring_pairs(count, lanes, step):
    rings = count // lanes
    return [(source, ((source // lanes - step) % rings) * lanes + source % lanes) for source in range(count)]


def exchange_rows(value, axis, count, lanes):
    index = lax.axis_index(axis)
    rings = count // lanes
    ring_index = index // lanes
    lane = index % lanes
    size = value.shape[0] // count
    received = [lax.dynamic_slice_in_dim(value, index * size, size, 0)]
    for step in range(1, rings):
        target = ((ring_index - step) % rings) * lanes + lane
        chunk = lax.dynamic_slice_in_dim(value, target * size, size, 0)
        received.append(lax.ppermute(chunk, axis, ring_pairs(count, lanes, step)))
    return unrotate(received, ring_index, value.shape[1])


def gather_columns(value, axis, count, lanes):
    ring_index = lax.axis_index(axis) // lanes
    received = [value] + [
        lax.ppermute(value, axis, ring_pairs(count, lanes, step)) for step in range(1, count // lanes)
    ]
    return unrotate(received, ring_index, value.shape[1])


def combine_stats(earlier, latter):
    new_max = jnp.maximum(earlier[0], latter[0])
    total = earlier[1] * jnp.exp(earlier[0] - new_max) + latter[1] * jnp.exp(latter[0] - new_max)
    return jnp.stack([new_max, total, earlier[2] + latter[2]])


def all_stats(stats, axis, count):
    step = 1
    while step < count:
        partner = lax.ppermute(stats, axis, [(source, source ^ step) for source in range(count)])
        stats = combine_stats(stats, partner)
        step *= 2
    return stats


def scatter_sum(value, axis, count):
    index = lax.axis_index(axis)
    size = value.shape[0] // count
    lanes = 2
    rings = count // lanes
    ring_index = index // lanes
    lane = index % lanes
    part = lax.dynamic_slice_in_dim(value, ring_index * lanes * size, lanes * size, 0)
    for step in range(1, rings):
        chunk = lax.dynamic_slice_in_dim(value, ((ring_index + step) % rings) * lanes * size, lanes * size, 0)
        pairs = [(source, ((source // lanes + step) % rings) * lanes + source % lanes) for source in range(count)]
        part = part + lax.ppermute(chunk, axis, pairs)
    other = lax.dynamic_slice_in_dim(part, (1 - lane) * size, size, 0)
    own = lax.dynamic_slice_in_dim(part, lane * size, size, 0)
    return own + lax.ppermute(other, axis, [(source, source ^ 1) for source in range(count)])


def body(queries, keys, projection, positives):
    rows = queries.shape[0]
    group_count = lax.axis_size("tensor")
    group_index = lax.axis_index("tensor")
    block_index = lax.axis_index("dp")
    slice_rows = rows // group_count
    row_start = group_index * slice_rows

    lanes = 2
    lane = group_index % lanes
    partner_projection = lax.ppermute(projection, "tensor", [(source, source ^ 1) for source in range(group_count)])

    def project(embeddings, weights):
        return jnp.dot(embeddings, weights, preferred_element_type=jnp.float32).astype(jnp.bfloat16)

    def paired(own, partner):
        return jnp.concatenate([jnp.where(lane == 0, own, partner), jnp.where(lane == 0, partner, own)], axis=1)

    key_own = project(keys, projection)
    query_own = project(queries, projection)
    key_part = paired(key_own, project(keys, partner_projection))
    query_part = paired(query_own, project(queries, partner_projection))
    key_rows = exchange_rows(key_part, "tensor", group_count, lanes)
    query_full = gather_columns(query_part, "tensor", group_count, lanes)

    query_unit, query_mag = normalize(query_full)
    queries_hat = query_unit.astype(jnp.bfloat16)
    key_unit, key_mag = normalize(key_rows)
    key_hat = key_unit.astype(jnp.bfloat16)
    keys_all = lax.all_gather(key_hat, "dp", axis=0, tiled=True)

    scores = SCALE * lax.dot_general(
        queries_hat, keys_all, (((1,), (1,)), ((), ())), preferred_element_type=jnp.float32
    )
    local_pos = positives[0] - row_start
    column = block_index * slice_rows + local_pos
    valid = (local_pos >= 0) & (local_pos < slice_rows)
    column = jnp.where(valid, column, -1)
    positive_mask = (
        lax.broadcasted_iota(jnp.int32, scores.shape, 1) == column[:, None]
    ).astype(jnp.float32)
    row_max = jnp.max(scores, axis=1)
    row_sum = jnp.sum(jnp.exp(scores - row_max[:, None]), axis=1)
    matched = jnp.sum(scores * positive_mask, axis=1)

    stats = all_stats(jnp.stack([row_max, row_sum, matched]), "tensor", group_count)
    matched = stats[2]
    log_total = stats[0] + jnp.log(stats[1])
    pair_loss = lax.dynamic_slice_in_dim(log_total - matched, row_start, slice_rows, 0)

    weights = (jnp.exp(scores - log_total[:, None]) - positive_mask).astype(jnp.bfloat16)
    grad_k = SCALE * lax.dot_general(
        weights, queries_hat, (((0,), (0,)), ((), ())), preferred_element_type=jnp.float32
    )
    grad_key_hat = lax.psum_scatter(grad_k, "dp", scatter_dimension=0, tiled=True)
    grad_q = SCALE * jnp.dot(weights, keys_all, preferred_element_type=jnp.float32)
    grad_rows = scatter_sum(grad_q, "tensor", group_count)

    unit_rows = lax.dynamic_slice_in_dim(query_unit, row_start, slice_rows, 0)
    magnitude_rows = lax.dynamic_slice_in_dim(query_mag, row_start, slice_rows, 0)
    grad_queries = unnormalize(grad_rows, unit_rows, magnitude_rows)
    grad_keys = unnormalize(grad_key_hat, key_unit, key_mag)
    return (pair_loss, grad_queries, grad_keys)


def solution(mesh):
    in_specs = (P("dp", None), P("dp", None), P(None, "tensor"), P("dp", None))
    out_specs = (P(("dp", "tensor")), P(("dp", "tensor"), None), P(("dp", "tensor"), None))
    return jax.shard_map(body, mesh=mesh, in_specs=in_specs, out_specs=out_specs, check_vma=False)
```

```python
import jax
import jax.numpy as jnp
from jax import lax
from jax.sharding import PartitionSpec as P

SCALE = 100.0
EPSILON = 1e-06


def normalize(embedding):
    entries = embedding.astype(jnp.float32)
    magnitude = jnp.sqrt(jnp.sum(entries * entries, axis=1, keepdims=True) + EPSILON)
    return (entries / magnitude, magnitude)


def unnormalize(grad_unit, unit_rows, magnitude):
    return (
        grad_unit - unit_rows * jnp.sum(unit_rows * grad_unit, axis=1, keepdims=True)
    ) / magnitude


def unrotate(pieces, index, width):
    count = len(pieces)
    return jnp.concatenate([lax.select_n((peer - index) % count, *pieces) for peer in range(count)], axis=1)


def ring_pairs(count, lanes, step):
    rings = count // lanes
    return [(source, ((source // lanes - step) % rings) * lanes + source % lanes) for source in range(count)]


def exchange_rows(value, axis, count, lanes):
    index = lax.axis_index(axis)
    rings = count // lanes
    ring_index = index // lanes
    lane = index % lanes
    size = value.shape[0] // count
    received = [lax.dynamic_slice_in_dim(value, index * size, size, 0)]
    for step in range(1, rings):
        target = ((ring_index - step) % rings) * lanes + lane
        chunk = lax.dynamic_slice_in_dim(value, target * size, size, 0)
        received.append(lax.ppermute(chunk, axis, ring_pairs(count, lanes, step)))
    return unrotate(received, ring_index, value.shape[1])


def gather_columns(value, axis, count, lanes):
    ring_index = lax.axis_index(axis) // lanes
    received = [value] + [
        lax.ppermute(value, axis, ring_pairs(count, lanes, step)) for step in range(1, count // lanes)
    ]
    return unrotate(received, ring_index, value.shape[1])


def combine_stats(earlier, latter):
    new_max = jnp.maximum(earlier[0], latter[0])
    total = earlier[1] * jnp.exp(earlier[0] - new_max) + latter[1] * jnp.exp(latter[0] - new_max)
    return jnp.stack([new_max, total, earlier[2] + latter[2]])


def all_stats(stats, axis, count):
    step = 1
    while step < count:
        partner = lax.ppermute(stats, axis, [(source, source ^ step) for source in range(count)])
        stats = combine_stats(stats, partner)
        step *= 2
    return stats


def scatter_sum(value, axis, count):
    index = lax.axis_index(axis)
    size = value.shape[0] // count
    lanes = 2
    rings = count // lanes
    ring_index = index // lanes
    lane = index % lanes
    part = lax.dynamic_slice_in_dim(value, ring_index * lanes * size, lanes * size, 0)
    for step in range(1, rings):
        chunk = lax.dynamic_slice_in_dim(value, ((ring_index + step) % rings) * lanes * size, lanes * size, 0)
        pairs = [(source, ((source // lanes + step) % rings) * lanes + source % lanes) for source in range(count)]
        part = part + lax.ppermute(chunk, axis, pairs)
    other = lax.dynamic_slice_in_dim(part, (1 - lane) * size, size, 0)
    own = lax.dynamic_slice_in_dim(part, lane * size, size, 0)
    return own + lax.ppermute(other, axis, [(source, source ^ 1) for source in range(count)])


def body(queries, keys, projection, positives):
    rows = queries.shape[0]
    group_count = lax.axis_size("tensor")
    group_index = lax.axis_index("tensor")
    block_index = lax.axis_index("dp")
    slice_rows = rows // group_count
    row_start = group_index * slice_rows

    lanes = 2
    lane = group_index % lanes
    partner_projection = lax.ppermute(projection, "tensor", [(source, source ^ 1) for source in range(group_count)])

    def project(embeddings, weights):
        return jnp.dot(embeddings, weights, preferred_element_type=jnp.float32).astype(jnp.bfloat16)

    def paired(own, partner):
        return jnp.concatenate([jnp.where(lane == 0, own, partner), jnp.where(lane == 0, partner, own)], axis=1)

    key_rows = exchange_rows(project(keys, projection), "tensor", group_count, 1)
    query_part = paired(project(queries, projection), project(queries, partner_projection))
    query_full = gather_columns(query_part, "tensor", group_count, lanes)

    query_unit, query_mag = normalize(query_full)
    queries_hat = query_unit.astype(jnp.bfloat16)
    key_unit, key_mag = normalize(key_rows)
    key_hat = key_unit.astype(jnp.bfloat16)
    keys_all = lax.all_gather(key_hat, "dp", axis=0, tiled=True)

    scores = SCALE * lax.dot_general(
        queries_hat, keys_all, (((1,), (1,)), ((), ())), preferred_element_type=jnp.float32
    )
    local_pos = positives[0] - row_start
    column = block_index * slice_rows + local_pos
    valid = (local_pos >= 0) & (local_pos < slice_rows)
    column = jnp.where(valid, column, -1)
    positive_mask = (
        lax.broadcasted_iota(jnp.int32, scores.shape, 1) == column[:, None]
    ).astype(jnp.float32)
    row_max = jnp.max(scores, axis=1)
    row_sum = jnp.sum(jnp.exp(scores - row_max[:, None]), axis=1)
    matched = jnp.sum(scores * positive_mask, axis=1)

    stats = all_stats(jnp.stack([row_max, row_sum, matched]), "tensor", group_count)
    matched = stats[2]
    log_total = stats[0] + jnp.log(stats[1])
    pair_loss = lax.dynamic_slice_in_dim(log_total - matched, row_start, slice_rows, 0)

    weights = (jnp.exp(scores - log_total[:, None]) - positive_mask).astype(jnp.bfloat16)
    grad_k = SCALE * lax.dot_general(
        weights, queries_hat, (((0,), (0,)), ((), ())), preferred_element_type=jnp.float32
    )
    grad_key_hat = lax.psum_scatter(grad_k, "dp", scatter_dimension=0, tiled=True)
    grad_q = SCALE * jnp.dot(weights, keys_all, preferred_element_type=jnp.float32)
    grad_rows = scatter_sum(grad_q, "tensor", group_count)

    unit_rows = lax.dynamic_slice_in_dim(query_unit, row_start, slice_rows, 0)
    magnitude_rows = lax.dynamic_slice_in_dim(query_mag, row_start, slice_rows, 0)
    grad_queries = unnormalize(grad_rows, unit_rows, magnitude_rows)
    grad_keys = unnormalize(grad_key_hat, key_unit, key_mag)
    return (pair_loss, grad_queries, grad_keys)


def solution(mesh):
    in_specs = (P("dp", None), P("dp", None), P(None, "tensor"), P("dp", None))
    out_specs = (P(("dp", "tensor")), P(("dp", "tensor"), None), P(("dp", "tensor"), None))
    return jax.shard_map(body, mesh=mesh, in_specs=in_specs, out_specs=out_specs, check_vma=False)
```

```python
import jax
import jax.numpy as jnp
from jax import lax
from jax.sharding import PartitionSpec as P

SCALE = 100.0
EPSILON = 1e-06


def normalize(embedding):
    entries = embedding.astype(jnp.float32)
    magnitude = jnp.sqrt(jnp.sum(entries * entries, axis=1, keepdims=True) + EPSILON)
    return (entries / magnitude, magnitude)


def unnormalize(grad_unit, unit_rows, magnitude):
    return (
        grad_unit - unit_rows * jnp.sum(unit_rows * grad_unit, axis=1, keepdims=True)
    ) / magnitude


def unrotate(pieces, index, width):
    count = len(pieces)
    return jnp.concatenate([lax.select_n((peer - index) % count, *pieces) for peer in range(count)], axis=1)


def ring_pairs(count, lanes, step):
    rings = count // lanes
    return [(source, ((source // lanes - step) % rings) * lanes + source % lanes) for source in range(count)]


def exchange_rows(value, axis, count, lanes):
    index = lax.axis_index(axis)
    rings = count // lanes
    ring_index = index // lanes
    lane = index % lanes
    size = value.shape[0] // count
    received = [lax.dynamic_slice_in_dim(value, index * size, size, 0)]
    for step in range(1, rings):
        target = ((ring_index - step) % rings) * lanes + lane
        chunk = lax.dynamic_slice_in_dim(value, target * size, size, 0)
        received.append(lax.ppermute(chunk, axis, ring_pairs(count, lanes, step)))
    return unrotate(received, ring_index, value.shape[1])


def gather_columns(value, axis, count, lanes):
    ring_index = lax.axis_index(axis) // lanes
    received = [value] + [
        lax.ppermute(value, axis, ring_pairs(count, lanes, step)) for step in range(1, count // lanes)
    ]
    return unrotate(received, ring_index, value.shape[1])


def combine_stats(earlier, latter):
    new_max = jnp.maximum(earlier[0], latter[0])
    total = earlier[1] * jnp.exp(earlier[0] - new_max) + latter[1] * jnp.exp(latter[0] - new_max)
    return jnp.stack([new_max, total, earlier[2] + latter[2]])


def all_stats(stats, axis, count):
    step = 1
    while step < count:
        partner = lax.ppermute(stats, axis, [(source, source ^ step) for source in range(count)])
        stats = combine_stats(stats, partner)
        step *= 2
    return stats


def scatter_sum(value, axis, count):
    index = lax.axis_index(axis)
    size = value.shape[0] // count
    lanes = 2
    rings = count // lanes
    ring_index = index // lanes
    lane = index % lanes
    part = lax.dynamic_slice_in_dim(value, ring_index * lanes * size, lanes * size, 0)
    for step in range(1, rings):
        chunk = lax.dynamic_slice_in_dim(value, ((ring_index + step) % rings) * lanes * size, lanes * size, 0)
        pairs = [(source, ((source // lanes + step) % rings) * lanes + source % lanes) for source in range(count)]
        part = part + lax.ppermute(chunk, axis, pairs)
    other = lax.dynamic_slice_in_dim(part, (1 - lane) * size, size, 0)
    own = lax.dynamic_slice_in_dim(part, lane * size, size, 0)
    return own + lax.ppermute(other, axis, [(source, source ^ 1) for source in range(count)])


def body(queries, keys, projection, positives):
    rows = queries.shape[0]
    group_count = lax.axis_size("tensor")
    group_index = lax.axis_index("tensor")
    block_index = lax.axis_index("dp")
    slice_rows = rows // group_count
    row_start = group_index * slice_rows

    lanes = 2
    lane = group_index % lanes
    partner_projection = lax.ppermute(projection, "tensor", [(source, source ^ 1) for source in range(group_count)])

    def project(embeddings, weights):
        return jnp.dot(embeddings, weights, preferred_element_type=jnp.float32).astype(jnp.bfloat16)

    def paired(own, partner):
        return jnp.concatenate([jnp.where(lane == 0, own, partner), jnp.where(lane == 0, partner, own)], axis=1)

    key_own = project(keys, projection)
    query_own = project(queries, projection)
    key_own, query_own, partner_projection = lax.optimization_barrier((key_own, query_own, partner_projection))
    key_rows = exchange_rows(key_own, "tensor", group_count, 1)
    query_part = paired(query_own, project(queries, partner_projection))
    query_full = gather_columns(query_part, "tensor", group_count, lanes)

    query_unit, query_mag = normalize(query_full)
    queries_hat = query_unit.astype(jnp.bfloat16)
    key_unit, key_mag = normalize(key_rows)
    key_hat = key_unit.astype(jnp.bfloat16)
    keys_all = lax.all_gather(key_hat, "dp", axis=0, tiled=True)

    scores = SCALE * lax.dot_general(
        queries_hat, keys_all, (((1,), (1,)), ((), ())), preferred_element_type=jnp.float32
    )
    local_pos = positives[0] - row_start
    column = block_index * slice_rows + local_pos
    valid = (local_pos >= 0) & (local_pos < slice_rows)
    column = jnp.where(valid, column, -1)
    positive_mask = (
        lax.broadcasted_iota(jnp.int32, scores.shape, 1) == column[:, None]
    ).astype(jnp.float32)
    row_max = jnp.max(scores, axis=1)
    row_sum = jnp.sum(jnp.exp(scores - row_max[:, None]), axis=1)
    matched = jnp.sum(scores * positive_mask, axis=1)

    stats = all_stats(jnp.stack([row_max, row_sum, matched]), "tensor", group_count)
    matched = stats[2]
    log_total = stats[0] + jnp.log(stats[1])
    pair_loss = lax.dynamic_slice_in_dim(log_total - matched, row_start, slice_rows, 0)

    weights = (jnp.exp(scores - log_total[:, None]) - positive_mask).astype(jnp.bfloat16)
    grad_k = SCALE * lax.dot_general(
        weights, queries_hat, (((0,), (0,)), ((), ())), preferred_element_type=jnp.float32
    )
    grad_key_hat = lax.psum_scatter(grad_k, "dp", scatter_dimension=0, tiled=True)
    grad_q = SCALE * jnp.dot(weights, keys_all, preferred_element_type=jnp.float32)
    grad_rows = scatter_sum(grad_q, "tensor", group_count)

    unit_rows = lax.dynamic_slice_in_dim(query_unit, row_start, slice_rows, 0)
    magnitude_rows = lax.dynamic_slice_in_dim(query_mag, row_start, slice_rows, 0)
    grad_queries = unnormalize(grad_rows, unit_rows, magnitude_rows)
    grad_keys = unnormalize(grad_key_hat, key_unit, key_mag)
    return (pair_loss, grad_queries, grad_keys)


def solution(mesh):
    in_specs = (P("dp", None), P("dp", None), P(None, "tensor"), P("dp", None))
    out_specs = (P(("dp", "tensor")), P(("dp", "tensor"), None), P(("dp", "tensor"), None))
    return jax.shard_map(body, mesh=mesh, in_specs=in_specs, out_specs=out_specs, check_vma=False)
```

```python
import jax
import jax.numpy as jnp
from jax import lax
from jax.sharding import PartitionSpec as P

SCALE = 100.0
EPSILON = 1e-06


def normalize(embedding):
    entries = embedding.astype(jnp.float32)
    magnitude = jnp.sqrt(jnp.sum(entries * entries, axis=1, keepdims=True) + EPSILON)
    return (entries / magnitude, magnitude)


def unnormalize(grad_unit, unit_rows, magnitude):
    return (
        grad_unit - unit_rows * jnp.sum(unit_rows * grad_unit, axis=1, keepdims=True)
    ) / magnitude


def unrotate(pieces, index, width):
    count = len(pieces)
    return jnp.concatenate([lax.select_n((peer - index) % count, *pieces) for peer in range(count)], axis=1)


def ring_pairs(count, lanes, step):
    rings = count // lanes
    return [(source, ((source // lanes - step) % rings) * lanes + source % lanes) for source in range(count)]


def exchange_rows(value, axis, count, lanes):
    index = lax.axis_index(axis)
    rings = count // lanes
    ring_index = index // lanes
    lane = index % lanes
    size = value.shape[0] // count
    received = [lax.dynamic_slice_in_dim(value, index * size, size, 0)]
    for step in range(1, rings):
        target = ((ring_index - step) % rings) * lanes + lane
        chunk = lax.dynamic_slice_in_dim(value, target * size, size, 0)
        received.append(lax.ppermute(chunk, axis, ring_pairs(count, lanes, step)))
    return unrotate(received, ring_index, value.shape[1])


def gather_columns(value, axis, count, lanes):
    ring_index = lax.axis_index(axis) // lanes
    received = [value] + [
        lax.ppermute(value, axis, ring_pairs(count, lanes, step)) for step in range(1, count // lanes)
    ]
    return unrotate(received, ring_index, value.shape[1])


def combine_stats(earlier, latter):
    new_max = jnp.maximum(earlier[0], latter[0])
    total = earlier[1] * jnp.exp(earlier[0] - new_max) + latter[1] * jnp.exp(latter[0] - new_max)
    return jnp.stack([new_max, total, earlier[2] + latter[2]])


def all_stats(stats, axis, count):
    step = 1
    while step < count:
        partner = lax.ppermute(stats, axis, [(source, source ^ step) for source in range(count)])
        stats = combine_stats(stats, partner)
        step *= 2
    return stats


def scatter_sum(value, axis, count):
    index = lax.axis_index(axis)
    size = value.shape[0] // count
    lanes = 2
    rings = count // lanes
    ring_index = index // lanes
    lane = index % lanes
    part = lax.dynamic_slice_in_dim(value, ring_index * lanes * size, lanes * size, 0)
    for step in range(1, rings):
        chunk = lax.dynamic_slice_in_dim(value, ((ring_index + step) % rings) * lanes * size, lanes * size, 0)
        pairs = [(source, ((source // lanes + step) % rings) * lanes + source % lanes) for source in range(count)]
        part = part + lax.ppermute(chunk, axis, pairs)
    other = lax.dynamic_slice_in_dim(part, (1 - lane) * size, size, 0)
    own = lax.dynamic_slice_in_dim(part, lane * size, size, 0)
    return own + lax.ppermute(other, axis, [(source, source ^ 1) for source in range(count)])


def body(queries, keys, projection, positives):
    rows = queries.shape[0]
    group_count = lax.axis_size("tensor")
    group_index = lax.axis_index("tensor")
    block_index = lax.axis_index("dp")
    slice_rows = rows // group_count
    row_start = group_index * slice_rows

    lanes = 2
    lane = group_index % lanes
    partner_projection = lax.ppermute(projection, "tensor", [(source, source ^ 1) for source in range(group_count)])

    def project(embeddings, weights):
        return jnp.dot(embeddings, weights, preferred_element_type=jnp.float32).astype(jnp.bfloat16)

    def paired(own, partner):
        return jnp.concatenate([jnp.where(lane == 0, own, partner), jnp.where(lane == 0, partner, own)], axis=1)

    key_rows = exchange_rows(project(keys, projection), "tensor", group_count, 1)
    query_own = project(queries, projection)
    key_rows, partner_projection = lax.optimization_barrier((key_rows, partner_projection))
    query_part = paired(query_own, project(queries, partner_projection))
    query_full = gather_columns(query_part, "tensor", group_count, lanes)

    query_unit, query_mag = normalize(query_full)
    queries_hat = query_unit.astype(jnp.bfloat16)
    key_unit, key_mag = normalize(key_rows)
    key_hat = key_unit.astype(jnp.bfloat16)
    keys_all = lax.all_gather(key_hat, "dp", axis=0, tiled=True)

    scores = SCALE * lax.dot_general(
        queries_hat, keys_all, (((1,), (1,)), ((), ())), preferred_element_type=jnp.float32
    )
    local_pos = positives[0] - row_start
    column = block_index * slice_rows + local_pos
    valid = (local_pos >= 0) & (local_pos < slice_rows)
    column = jnp.where(valid, column, -1)
    positive_mask = (
        lax.broadcasted_iota(jnp.int32, scores.shape, 1) == column[:, None]
    ).astype(jnp.float32)
    row_max = jnp.max(scores, axis=1)
    row_sum = jnp.sum(jnp.exp(scores - row_max[:, None]), axis=1)
    matched = jnp.sum(scores * positive_mask, axis=1)

    stats = all_stats(jnp.stack([row_max, row_sum, matched]), "tensor", group_count)
    matched = stats[2]
    log_total = stats[0] + jnp.log(stats[1])
    pair_loss = lax.dynamic_slice_in_dim(log_total - matched, row_start, slice_rows, 0)

    weights = (jnp.exp(scores - log_total[:, None]) - positive_mask).astype(jnp.bfloat16)
    grad_k = SCALE * lax.dot_general(
        weights, queries_hat, (((0,), (0,)), ((), ())), preferred_element_type=jnp.float32
    )
    grad_key_hat = lax.psum_scatter(grad_k, "dp", scatter_dimension=0, tiled=True)
    grad_q = SCALE * jnp.dot(weights, keys_all, preferred_element_type=jnp.float32)
    grad_rows = scatter_sum(grad_q, "tensor", group_count)

    unit_rows = lax.dynamic_slice_in_dim(query_unit, row_start, slice_rows, 0)
    magnitude_rows = lax.dynamic_slice_in_dim(query_mag, row_start, slice_rows, 0)
    grad_queries = unnormalize(grad_rows, unit_rows, magnitude_rows)
    grad_keys = unnormalize(grad_key_hat, key_unit, key_mag)
    return (pair_loss, grad_queries, grad_keys)


def solution(mesh):
    in_specs = (P("dp", None), P("dp", None), P(None, "tensor"), P("dp", None))
    out_specs = (P(("dp", "tensor")), P(("dp", "tensor"), None), P(("dp", "tensor"), None))
    return jax.shard_map(body, mesh=mesh, in_specs=in_specs, out_specs=out_specs, check_vma=False)
```

```python
import jax
import jax.numpy as jnp
from jax import lax
from jax.sharding import PartitionSpec as P

SCALE = 100.0
EPSILON = 1e-06


def normalize(embedding):
    entries = embedding.astype(jnp.float32)
    magnitude = jnp.sqrt(jnp.sum(entries * entries, axis=1, keepdims=True) + EPSILON)
    return (entries / magnitude, magnitude)


def unnormalize(grad_unit, unit_rows, magnitude):
    return (
        grad_unit - unit_rows * jnp.sum(unit_rows * grad_unit, axis=1, keepdims=True)
    ) / magnitude


def unrotate(pieces, index, width):
    count = len(pieces)
    return jnp.concatenate([lax.select_n((peer - index) % count, *pieces) for peer in range(count)], axis=1)


def ring_pairs(count, lanes, step):
    rings = count // lanes
    return [(source, ((source // lanes - step) % rings) * lanes + source % lanes) for source in range(count)]


def exchange_rows(value, axis, count, lanes):
    index = lax.axis_index(axis)
    rings = count // lanes
    ring_index = index // lanes
    lane = index % lanes
    size = value.shape[0] // count
    received = [lax.dynamic_slice_in_dim(value, index * size, size, 0)]
    for step in range(1, rings):
        target = ((ring_index - step) % rings) * lanes + lane
        chunk = lax.dynamic_slice_in_dim(value, target * size, size, 0)
        received.append(lax.ppermute(chunk, axis, ring_pairs(count, lanes, step)))
    return unrotate(received, ring_index, value.shape[1])


def gather_columns(value, axis, count, lanes):
    ring_index = lax.axis_index(axis) // lanes
    received = [value] + [
        lax.ppermute(value, axis, ring_pairs(count, lanes, step)) for step in range(1, count // lanes)
    ]
    return unrotate(received, ring_index, value.shape[1])


def combine_stats(earlier, latter):
    new_max = jnp.maximum(earlier[0], latter[0])
    total = earlier[1] * jnp.exp(earlier[0] - new_max) + latter[1] * jnp.exp(latter[0] - new_max)
    return jnp.stack([new_max, total, earlier[2] + latter[2]])


def all_stats(stats, axis, count):
    step = 1
    while step < count:
        partner = lax.ppermute(stats, axis, [(source, source ^ step) for source in range(count)])
        stats = combine_stats(stats, partner)
        step *= 2
    return stats


def scatter_sum(value, axis, count):
    index = lax.axis_index(axis)
    size = value.shape[0] // count
    lanes = 2
    rings = count // lanes
    ring_index = index // lanes
    lane = index % lanes
    part = lax.dynamic_slice_in_dim(value, ring_index * lanes * size, lanes * size, 0)
    for step in range(1, rings):
        chunk = lax.dynamic_slice_in_dim(value, ((ring_index + step) % rings) * lanes * size, lanes * size, 0)
        pairs = [(source, ((source // lanes + step) % rings) * lanes + source % lanes) for source in range(count)]
        part = part + lax.ppermute(chunk, axis, pairs)
    other = lax.dynamic_slice_in_dim(part, (1 - lane) * size, size, 0)
    own = lax.dynamic_slice_in_dim(part, lane * size, size, 0)
    return own + lax.ppermute(other, axis, [(source, source ^ 1) for source in range(count)])


def body(queries, keys, projection, positives):
    rows = queries.shape[0]
    group_count = lax.axis_size("tensor")
    group_index = lax.axis_index("tensor")
    block_index = lax.axis_index("dp")
    slice_rows = rows // group_count
    row_start = group_index * slice_rows

    lanes = 2
    lane = group_index % lanes
    partner_projection = lax.ppermute(projection, "tensor", [(source, source ^ 1) for source in range(group_count)])

    def project(embeddings, weights):
        return jnp.dot(embeddings, weights, preferred_element_type=jnp.float32).astype(jnp.bfloat16)

    def paired(own, partner):
        return jnp.concatenate([jnp.where(lane == 0, own, partner), jnp.where(lane == 0, partner, own)], axis=1)

    key_own = project(keys, projection)
    query_own = project(queries, projection)
    key_own, query_own, partner_projection = lax.optimization_barrier((key_own, query_own, partner_projection))
    key_rows = lax.all_to_all(key_own, "tensor", 0, 1, tiled=True)
    query_part = paired(query_own, project(queries, partner_projection))
    query_full = gather_columns(query_part, "tensor", group_count, lanes)

    query_unit, query_mag = normalize(query_full)
    queries_hat = query_unit.astype(jnp.bfloat16)
    key_unit, key_mag = normalize(key_rows)
    key_hat = key_unit.astype(jnp.bfloat16)
    keys_all = lax.all_gather(key_hat, "dp", axis=0, tiled=True)

    scores = SCALE * lax.dot_general(
        queries_hat, keys_all, (((1,), (1,)), ((), ())), preferred_element_type=jnp.float32
    )
    local_pos = positives[0] - row_start
    column = block_index * slice_rows + local_pos
    valid = (local_pos >= 0) & (local_pos < slice_rows)
    column = jnp.where(valid, column, -1)
    positive_mask = (
        lax.broadcasted_iota(jnp.int32, scores.shape, 1) == column[:, None]
    ).astype(jnp.float32)
    row_max = jnp.max(scores, axis=1)
    row_sum = jnp.sum(jnp.exp(scores - row_max[:, None]), axis=1)
    matched = jnp.sum(scores * positive_mask, axis=1)

    stats = all_stats(jnp.stack([row_max, row_sum, matched]), "tensor", group_count)
    matched = stats[2]
    log_total = stats[0] + jnp.log(stats[1])
    pair_loss = lax.dynamic_slice_in_dim(log_total - matched, row_start, slice_rows, 0)

    weights = (jnp.exp(scores - log_total[:, None]) - positive_mask).astype(jnp.bfloat16)
    grad_k = SCALE * lax.dot_general(
        weights, queries_hat, (((0,), (0,)), ((), ())), preferred_element_type=jnp.float32
    )
    grad_key_hat = lax.psum_scatter(grad_k, "dp", scatter_dimension=0, tiled=True)
    grad_q = SCALE * jnp.dot(weights, keys_all, preferred_element_type=jnp.float32)
    grad_rows = scatter_sum(grad_q, "tensor", group_count)

    unit_rows = lax.dynamic_slice_in_dim(query_unit, row_start, slice_rows, 0)
    magnitude_rows = lax.dynamic_slice_in_dim(query_mag, row_start, slice_rows, 0)
    grad_queries = unnormalize(grad_rows, unit_rows, magnitude_rows)
    grad_keys = unnormalize(grad_key_hat, key_unit, key_mag)
    return (pair_loss, grad_queries, grad_keys)


def solution(mesh):
    in_specs = (P("dp", None), P("dp", None), P(None, "tensor"), P("dp", None))
    out_specs = (P(("dp", "tensor")), P(("dp", "tensor"), None), P(("dp", "tensor"), None))
    return jax.shard_map(body, mesh=mesh, in_specs=in_specs, out_specs=out_specs, check_vma=False)
```

```python
import jax
import jax.numpy as jnp
from jax import lax
from jax.sharding import PartitionSpec as P

SCALE = 100.0
EPSILON = 1e-06


def normalize(embedding):
    entries = embedding.astype(jnp.float32)
    magnitude = jnp.sqrt(jnp.sum(entries * entries, axis=1, keepdims=True) + EPSILON)
    return (entries / magnitude, magnitude)


def unnormalize(grad_unit, unit_rows, magnitude):
    return (
        grad_unit - unit_rows * jnp.sum(unit_rows * grad_unit, axis=1, keepdims=True)
    ) / magnitude


def unrotate(pieces, index, width):
    count = len(pieces)
    return jnp.concatenate([lax.select_n((peer - index) % count, *pieces) for peer in range(count)], axis=1)


def ring_pairs(count, lanes, step):
    rings = count // lanes
    return [(source, ((source // lanes - step) % rings) * lanes + source % lanes) for source in range(count)]


def gather_columns(value, axis, count, lanes):
    ring_index = lax.axis_index(axis) // lanes
    received = [value] + [
        lax.ppermute(value, axis, ring_pairs(count, lanes, step)) for step in range(1, count // lanes)
    ]
    return unrotate(received, ring_index, value.shape[1])


def combine_stats(earlier, latter):
    new_max = jnp.maximum(earlier[0], latter[0])
    total = earlier[1] * jnp.exp(earlier[0] - new_max) + latter[1] * jnp.exp(latter[0] - new_max)
    return jnp.stack([new_max, total, earlier[2] + latter[2]])


def all_stats(stats, axis, count):
    step = 1
    while step < count:
        partner = lax.ppermute(stats, axis, [(source, source ^ step) for source in range(count)])
        stats = combine_stats(stats, partner)
        step *= 2
    return stats


def scatter_sum(value, axis, count):
    index = lax.axis_index(axis)
    size = value.shape[0] // count
    lanes = 2
    rings = count // lanes
    ring_index = index // lanes
    lane = index % lanes
    part = lax.dynamic_slice_in_dim(value, ring_index * lanes * size, lanes * size, 0)
    for step in range(1, rings):
        chunk = lax.dynamic_slice_in_dim(value, ((ring_index + step) % rings) * lanes * size, lanes * size, 0)
        pairs = [(source, ((source // lanes + step) % rings) * lanes + source % lanes) for source in range(count)]
        part = part + lax.ppermute(chunk, axis, pairs)
    other = lax.dynamic_slice_in_dim(part, (1 - lane) * size, size, 0)
    own = lax.dynamic_slice_in_dim(part, lane * size, size, 0)
    return own + lax.ppermute(other, axis, [(source, source ^ 1) for source in range(count)])


def body(queries, keys, projection, positives):
    rows = queries.shape[0]
    group_count = lax.axis_size("tensor")
    group_index = lax.axis_index("tensor")
    block_index = lax.axis_index("dp")
    slice_rows = rows // group_count
    row_start = group_index * slice_rows

    lanes = 2
    lane = group_index % lanes
    partner_projection = lax.ppermute(projection, "tensor", [(source, source ^ 1) for source in range(group_count)])

    def project(embeddings, weights):
        return jnp.dot(embeddings, weights, preferred_element_type=jnp.float32).astype(jnp.bfloat16)

    def paired(own, partner):
        return jnp.concatenate([jnp.where(lane == 0, own, partner), jnp.where(lane == 0, partner, own)], axis=1)

    key_rows = lax.all_to_all(project(keys, projection), "tensor", 0, 1, tiled=True)
    query_own = project(queries, projection)
    key_rows, query_own, partner_projection = lax.optimization_barrier((key_rows, query_own, partner_projection))
    query_part = paired(query_own, project(queries, partner_projection))
    query_full = gather_columns(query_part, "tensor", group_count, lanes)

    query_unit, query_mag = normalize(query_full)
    queries_hat = query_unit.astype(jnp.bfloat16)
    key_unit, key_mag = normalize(key_rows)
    key_hat = key_unit.astype(jnp.bfloat16)
    keys_all = lax.all_gather(key_hat, "dp", axis=0, tiled=True)

    scores = SCALE * lax.dot_general(
        queries_hat, keys_all, (((1,), (1,)), ((), ())), preferred_element_type=jnp.float32
    )
    local_pos = positives[0] - row_start
    column = block_index * slice_rows + local_pos
    valid = (local_pos >= 0) & (local_pos < slice_rows)
    column = jnp.where(valid, column, -1)
    positive_mask = (
        lax.broadcasted_iota(jnp.int32, scores.shape, 1) == column[:, None]
    ).astype(jnp.float32)
    row_max = jnp.max(scores, axis=1)
    row_sum = jnp.sum(jnp.exp(scores - row_max[:, None]), axis=1)
    matched = jnp.sum(scores * positive_mask, axis=1)

    stats = all_stats(jnp.stack([row_max, row_sum, matched]), "tensor", group_count)
    matched = stats[2]
    log_total = stats[0] + jnp.log(stats[1])
    pair_loss = lax.dynamic_slice_in_dim(log_total - matched, row_start, slice_rows, 0)

    weights = (jnp.exp(scores - log_total[:, None]) - positive_mask).astype(jnp.bfloat16)
    grad_k = SCALE * lax.dot_general(
        weights, queries_hat, (((0,), (0,)), ((), ())), preferred_element_type=jnp.float32
    )
    grad_key_hat = lax.psum_scatter(grad_k, "dp", scatter_dimension=0, tiled=True)
    grad_q = SCALE * jnp.dot(weights, keys_all, preferred_element_type=jnp.float32)
    grad_rows = scatter_sum(grad_q, "tensor", group_count)

    unit_rows = lax.dynamic_slice_in_dim(query_unit, row_start, slice_rows, 0)
    magnitude_rows = lax.dynamic_slice_in_dim(query_mag, row_start, slice_rows, 0)
    grad_queries = unnormalize(grad_rows, unit_rows, magnitude_rows)
    grad_keys = unnormalize(grad_key_hat, key_unit, key_mag)
    return (pair_loss, grad_queries, grad_keys)


def solution(mesh):
    in_specs = (P("dp", None), P("dp", None), P(None, "tensor"), P("dp", None))
    out_specs = (P(("dp", "tensor")), P(("dp", "tensor"), None), P(("dp", "tensor"), None))
    return jax.shard_map(body, mesh=mesh, in_specs=in_specs, out_specs=out_specs, check_vma=False)
```

```python
import jax
import jax.numpy as jnp
from jax import lax
from jax.sharding import PartitionSpec as P

SCALE = 100.0
EPSILON = 1e-06


def normalize(embedding):
    entries = embedding.astype(jnp.float32)
    magnitude = jnp.sqrt(jnp.sum(entries * entries, axis=1, keepdims=True) + EPSILON)
    return (entries / magnitude, magnitude)


def unnormalize(grad_unit, unit_rows, magnitude):
    return (
        grad_unit - unit_rows * jnp.sum(unit_rows * grad_unit, axis=1, keepdims=True)
    ) / magnitude


def unrotate(pieces, index, width):
    count = len(pieces)
    return jnp.concatenate([lax.select_n((peer - index) % count, *pieces) for peer in range(count)], axis=1)


def ring_pairs(count, lanes, step):
    rings = count // lanes
    return [(source, ((source // lanes - step) % rings) * lanes + source % lanes) for source in range(count)]


def gather_columns(value, axis, count, lanes):
    ring_index = lax.axis_index(axis) // lanes
    received = [value] + [
        lax.ppermute(value, axis, ring_pairs(count, lanes, step)) for step in range(1, count // lanes)
    ]
    return unrotate(received, ring_index, value.shape[1])


def combine_stats(earlier, latter):
    new_max = jnp.maximum(earlier[0], latter[0])
    total = earlier[1] * jnp.exp(earlier[0] - new_max) + latter[1] * jnp.exp(latter[0] - new_max)
    return jnp.stack([new_max, total, earlier[2] + latter[2]])


def all_stats(stats, axis, count):
    step = 1
    while step < count:
        partner = lax.ppermute(stats, axis, [(source, source ^ step) for source in range(count)])
        stats = combine_stats(stats, partner)
        step *= 2
    return stats


def scatter_sum(value, axis, count):
    index = lax.axis_index(axis)
    size = value.shape[0] // count
    lanes = 2
    rings = count // lanes
    ring_index = index // lanes
    lane = index % lanes
    part = lax.dynamic_slice_in_dim(value, ring_index * lanes * size, lanes * size, 0)
    for step in range(1, rings):
        chunk = lax.dynamic_slice_in_dim(value, ((ring_index + step) % rings) * lanes * size, lanes * size, 0)
        pairs = [(source, ((source // lanes + step) % rings) * lanes + source % lanes) for source in range(count)]
        part = part + lax.ppermute(chunk, axis, pairs)
    other = lax.dynamic_slice_in_dim(part, (1 - lane) * size, size, 0)
    own = lax.dynamic_slice_in_dim(part, lane * size, size, 0)
    return own + lax.ppermute(other, axis, [(source, source ^ 1) for source in range(count)])


def body(queries, keys, projection, positives):
    rows = queries.shape[0]
    group_count = lax.axis_size("tensor")
    group_index = lax.axis_index("tensor")
    block_index = lax.axis_index("dp")
    slice_rows = rows // group_count
    row_start = group_index * slice_rows

    lanes = 2
    lane = group_index % lanes
    partner_projection = lax.ppermute(projection, "tensor", [(source, source ^ 1) for source in range(group_count)])

    def project(embeddings, weights):
        return jnp.dot(embeddings, weights, preferred_element_type=jnp.float32).astype(jnp.bfloat16)

    def paired(own, partner):
        return jnp.concatenate([jnp.where(lane == 0, own, partner), jnp.where(lane == 0, partner, own)], axis=1)

    key_rows = lax.all_to_all(project(keys, projection), "tensor", 0, 1, tiled=True)
    query_own = project(queries, projection)
    key_rows, query_own, partner_projection = lax.optimization_barrier((key_rows, query_own, partner_projection))
    query_part = paired(query_own, project(queries, partner_projection))
    query_full = gather_columns(query_part, "tensor", group_count, lanes)

    query_unit, query_mag = normalize(query_full)
    queries_hat = query_unit.astype(jnp.bfloat16)
    key_unit, key_mag = normalize(key_rows)
    key_hat = key_unit.astype(jnp.bfloat16)
    keys_all = lax.all_gather(key_hat, "dp", axis=0, tiled=True)

    scores = SCALE * lax.dot_general(
        queries_hat, keys_all, (((1,), (1,)), ((), ())), preferred_element_type=jnp.float32
    )
    local_pos = positives[0] - row_start
    column = block_index * slice_rows + local_pos
    valid = (local_pos >= 0) & (local_pos < slice_rows)
    column = jnp.where(valid, column, -1)
    positive_mask = (
        lax.broadcasted_iota(jnp.int32, scores.shape, 1) == column[:, None]
    ).astype(jnp.float32)
    row_max = jnp.max(scores, axis=1)
    row_sum = jnp.sum(jnp.exp(scores - row_max[:, None]), axis=1)
    matched = jnp.sum(scores * positive_mask, axis=1)

    stats = all_stats(jnp.stack([row_max, row_sum, matched]), "tensor", group_count)
    matched = stats[2]
    log_total = stats[0] + jnp.log(stats[1])
    pair_loss = lax.dynamic_slice_in_dim(log_total - matched, row_start, slice_rows, 0)

    weights = (jnp.exp(scores - log_total[:, None]) - positive_mask).astype(jnp.bfloat16)
    half = queries_hat.shape[1] // 2
    grad_key_hat = jnp.concatenate([
        lax.psum_scatter(
            SCALE * lax.dot_general(
                weights, columns, (((0,), (0,)), ((), ())), preferred_element_type=jnp.float32
            ),
            "dp", scatter_dimension=0, tiled=True,
        )
        for columns in (queries_hat[:, :half], queries_hat[:, half:])
    ], axis=1)
    grad_q = SCALE * jnp.dot(weights, keys_all, preferred_element_type=jnp.float32)
    grad_rows = scatter_sum(grad_q, "tensor", group_count)

    unit_rows = lax.dynamic_slice_in_dim(query_unit, row_start, slice_rows, 0)
    magnitude_rows = lax.dynamic_slice_in_dim(query_mag, row_start, slice_rows, 0)
    grad_queries = unnormalize(grad_rows, unit_rows, magnitude_rows)
    grad_keys = unnormalize(grad_key_hat, key_unit, key_mag)
    return (pair_loss, grad_queries, grad_keys)


def solution(mesh):
    in_specs = (P("dp", None), P("dp", None), P(None, "tensor"), P("dp", None))
    out_specs = (P(("dp", "tensor")), P(("dp", "tensor"), None), P(("dp", "tensor"), None))
    return jax.shard_map(body, mesh=mesh, in_specs=in_specs, out_specs=out_specs, check_vma=False)
```

```python
import jax
import jax.numpy as jnp
from jax import lax
from jax.sharding import PartitionSpec as P

SCALE = 100.0
EPSILON = 1e-06


def normalize(embedding):
    entries = embedding.astype(jnp.float32)
    magnitude = jnp.sqrt(jnp.sum(entries * entries, axis=1, keepdims=True) + EPSILON)
    return (entries / magnitude, magnitude)


def unnormalize(grad_unit, unit_rows, magnitude):
    return (
        grad_unit - unit_rows * jnp.sum(unit_rows * grad_unit, axis=1, keepdims=True)
    ) / magnitude


def unrotate(pieces, index, width):
    count = len(pieces)
    return jnp.concatenate([lax.select_n((peer - index) % count, *pieces) for peer in range(count)], axis=1)


def ring_pairs(count, lanes, step):
    rings = count // lanes
    return [(source, ((source // lanes - step) % rings) * lanes + source % lanes) for source in range(count)]


def gather_columns(value, axis, count, lanes):
    ring_index = lax.axis_index(axis) // lanes
    received = [value] + [
        lax.ppermute(value, axis, ring_pairs(count, lanes, step)) for step in range(1, count // lanes)
    ]
    return unrotate(received, ring_index, value.shape[1])


def combine_stats(earlier, latter):
    new_max = jnp.maximum(earlier[0], latter[0])
    total = earlier[1] * jnp.exp(earlier[0] - new_max) + latter[1] * jnp.exp(latter[0] - new_max)
    return jnp.stack([new_max, total, earlier[2] + latter[2]])


def all_stats(stats, axis, count):
    step = 1
    while step < count:
        partner = lax.ppermute(stats, axis, [(source, source ^ step) for source in range(count)])
        stats = combine_stats(stats, partner)
        step *= 2
    return stats


def scatter_sum(value, axis, count):
    index = lax.axis_index(axis)
    size = value.shape[0] // count
    lanes = 2
    rings = count // lanes
    ring_index = index // lanes
    lane = index % lanes
    part = lax.dynamic_slice_in_dim(value, ring_index * lanes * size, lanes * size, 0)
    for step in range(1, rings):
        chunk = lax.dynamic_slice_in_dim(value, ((ring_index + step) % rings) * lanes * size, lanes * size, 0)
        pairs = [(source, ((source // lanes + step) % rings) * lanes + source % lanes) for source in range(count)]
        part = part + lax.ppermute(chunk, axis, pairs)
    other = lax.dynamic_slice_in_dim(part, (1 - lane) * size, size, 0)
    own = lax.dynamic_slice_in_dim(part, lane * size, size, 0)
    return own + lax.ppermute(other, axis, [(source, source ^ 1) for source in range(count)])


def body(queries, keys, projection, positives):
    rows = queries.shape[0]
    group_count = lax.axis_size("tensor")
    group_index = lax.axis_index("tensor")
    block_index = lax.axis_index("dp")
    slice_rows = rows // group_count
    row_start = group_index * slice_rows

    lanes = 2
    lane = group_index % lanes
    partner_projection = lax.ppermute(projection, "tensor", [(source, source ^ 1) for source in range(group_count)])

    def project(embeddings, weights):
        return jnp.dot(embeddings, weights, preferred_element_type=jnp.float32).astype(jnp.bfloat16)

    def paired(own, partner):
        return jnp.concatenate([jnp.where(lane == 0, own, partner), jnp.where(lane == 0, partner, own)], axis=1)

    key_rows = lax.all_to_all(project(keys, projection), "tensor", 0, 1, tiled=True)
    query_own = project(queries, projection)
    key_rows, query_own, partner_projection = lax.optimization_barrier((key_rows, query_own, partner_projection))
    query_part = paired(query_own, project(queries, partner_projection))
    query_full = gather_columns(query_part, "tensor", group_count, lanes)

    query_unit, query_mag = normalize(query_full)
    queries_hat = query_unit.astype(jnp.bfloat16)
    key_unit, key_mag = normalize(key_rows)
    key_hat = key_unit.astype(jnp.bfloat16)
    keys_all = lax.all_gather(key_hat, "dp", axis=0, tiled=True)

    scores = SCALE * lax.dot_general(
        keys_all, queries_hat, (((1,), (1,)), ((), ())), preferred_element_type=jnp.float32
    )
    local_pos = positives[0] - row_start
    column = block_index * slice_rows + local_pos
    valid = (local_pos >= 0) & (local_pos < slice_rows)
    column = jnp.where(valid, column, -1)
    positive_mask = (
        lax.broadcasted_iota(jnp.int32, scores.shape, 0) == column[None, :]
    ).astype(jnp.float32)
    row_max = jnp.max(scores, axis=0)
    row_sum = jnp.sum(jnp.exp(scores - row_max[None, :]), axis=0)
    matched = jnp.sum(scores * positive_mask, axis=0)

    stats = all_stats(jnp.stack([row_max, row_sum, matched]), "tensor", group_count)
    matched = stats[2]
    log_total = stats[0] + jnp.log(stats[1])
    pair_loss = lax.dynamic_slice_in_dim(log_total - matched, row_start, slice_rows, 0)

    weights = (jnp.exp(scores - log_total[None, :]) - positive_mask).astype(jnp.bfloat16)
    grad_k = SCALE * jnp.dot(weights, queries_hat, preferred_element_type=jnp.float32)
    grad_key_hat = lax.psum_scatter(grad_k, "dp", scatter_dimension=0, tiled=True)
    grad_q = SCALE * lax.dot_general(
        weights, keys_all, (((0,), (0,)), ((), ())), preferred_element_type=jnp.float32
    )
    grad_rows = scatter_sum(grad_q, "tensor", group_count)

    unit_rows = lax.dynamic_slice_in_dim(query_unit, row_start, slice_rows, 0)
    magnitude_rows = lax.dynamic_slice_in_dim(query_mag, row_start, slice_rows, 0)
    grad_queries = unnormalize(grad_rows, unit_rows, magnitude_rows)
    grad_keys = unnormalize(grad_key_hat, key_unit, key_mag)
    return (pair_loss, grad_queries, grad_keys)


def solution(mesh):
    in_specs = (P("dp", None), P("dp", None), P(None, "tensor"), P("dp", None))
    out_specs = (P(("dp", "tensor")), P(("dp", "tensor"), None), P(("dp", "tensor"), None))
    return jax.shard_map(body, mesh=mesh, in_specs=in_specs, out_specs=out_specs, check_vma=False)
```
